768 devices in a mesh: fsdp: 96 (over x, y_lo, z), island: 8 (over y_hi, core).
Axes of the slice: x: 4, y: 8 (y_hi: 4, y_lo: 2; y = y_hi * 2 + y_lo), z: 12, core: 2. Of those that a mesh axis runs over, the one named last changes fastest.
Arguments:
- acts: bfloat16 [8, 24576, 4096], P('island', 'fsdp'), may hold values from -6 to 6
- grad_out: bfloat16 [8, 24576, 128], P('island', 'fsdp'), may hold values from -0.15234375 to 0.15234375
- params: float32 [8, 4128, 128], P('island', 'fsdp'), may hold values from -3 to 3
- adam_m: float32 [8, 4128, 128], P('island', 'fsdp'), may hold values from -4 to 4
- adam_v: float32 [8, 4128, 128], P('island', 'fsdp'), may hold values from 0.01 to 16
- global_params: float32 [4128, 128], P('fsdp'), may hold values from -3 to 3
- outer_mom: float32 [4128, 128], P('fsdp'), may hold values from -2 to 2
Outputs:
- mixed: float32 [8, 4128, 128], P('island', 'fsdp')
- first_moment: float32 [8, 4128, 128], P('island', 'fsdp')
- second_moment: float32 [8, 4128, 128], P('island', 'fsdp')
- new_global: float32 [4128, 128], P('fsdp')
- new_mom: float32 [4128, 128], P('fsdp')
- forward_weight: bfloat16 [8, 4096, 128], P('island')
The draws below stay inside these ranges and needn't reach their ends.
All inputs are finite; a program needn't handle non-finite values.
Results may differ from the reference program's by a relative error of at most 0.0004.
Values may be sent and summed in bfloat16 or wider, within the bound.
No kernel may reach another device: no remote copies, remote signals or barrier semaphores. Data moves between devices by JAX's collectives and lax.ppermute only.
A program may use at most 32 MiB of HBM per device.

```python
import math
import jax
import jax.numpy as jnp
from jax import lax

D = 4096
HD = 128
INNER_STEP = 100
ISLANDS = 8
TOKENS = 24576
DP = 4128


def steps_of(rng, extent, cuts, least, largest):
    gain, own = 1.0, jax.random.fold_in(rng, 6)
    for axis_at, blocks in cuts:
        heights = jnp.exp(jax.random.uniform(jax.random.fold_in(own, axis_at), (blocks,), jnp.float32, least / len(cuts), largest / len(cuts)))
        gain = gain * jnp.repeat(heights, extent[axis_at] // blocks).reshape([-1 if axis == axis_at else 1 for axis in range(len(extent))])
    return gain


def centred(own_key, extent, scale, bound, shards=(), kind=jnp.bfloat16):
    result = jax.random.normal(own_key, extent, jnp.float32) * scale
    if len(shards) > 0:
        result = steps_of(own_key, extent, shards, -0.22, 0.18) * result
    return jnp.clip(result, min=-bound, max=bound).astype(kind)


def setup_inputs(seed: int = 0) -> dict:
    key_of = jax.random.split(jax.random.key(seed), 8)
    return {
        "acts": centred(key_of[0], (ISLANDS, TOKENS, D), 1.0, 6.0, ((0, 8), (1, 96))),
        "grad_out": centred(key_of[1], (ISLANDS, TOKENS, HD), (4.0 * TOKENS ** -0.5), 0.15234375, ((0, 8), (1, 96))),
        "params": centred(key_of[2], (ISLANDS, DP, HD), 0.5, 3.0, ((0, 8), (1, 96)), jnp.float32),
        "adam_m": centred(key_of[3], (ISLANDS, DP, HD), 1.0, 4.0, ((0, 8), (1, 96)), jnp.float32),
        "adam_v": jnp.clip(jnp.exp(math.log(16.0) - 7.377759 * jax.random.uniform(key_of[4], (ISLANDS, DP, HD), jnp.float32) ** steps_of(key_of[4], (ISLANDS, DP, HD), ((0, 8), (1, 96)), -0.2, 0.2)), 0.01, 16.0),
        "global_params": centred(key_of[5], (DP, HD), 0.5, 3.0, ((0, 96),), jnp.float32),
        "outer_mom": centred(key_of[6], (DP, HD), 0.3, 2.0, ((0, 96),), jnp.float32),
    }


beta_one = 0.9
beta_two = 0.95
epsilon = 1e-08
inner_rate = 0.001
decay_rate = 0.1
outer_rate = 0.7
momentum = 0.9
mixing = 0.5

def island_gradient(pair):
    inputs, cotangent = pair
    return jnp.dot(inputs.T, cotangent, preferred_element_type=jnp.float32)

def reference(acts, grad_out, params, adam_m, adam_v, global_params, outer_mom):
    gradient = lax.map(island_gradient, (acts, grad_out))
    padding = params.shape[1] - gradient.shape[1]
    gradient = jnp.pad(gradient, ((0, 0), (0, padding), (0, 0)))
    first_moment = beta_one * adam_m + (1.0 - beta_one) * gradient
    second_moment = beta_two * adam_v + (1.0 - beta_two) * gradient * gradient
    first_hat = first_moment / (1.0 - beta_one ** INNER_STEP)
    second_hat = second_moment / (1.0 - beta_two ** INNER_STEP)
    inner = params - inner_rate * (first_hat / (jnp.sqrt(second_hat) + epsilon) + decay_rate * params)
    delta = lax.optimization_barrier(jnp.sum(global_params[None] - inner, axis=0)) / ISLANDS
    new_mom = momentum * outer_mom + delta
    new_global = global_params - outer_rate * (delta + momentum * new_mom)
    mixed = mixing * inner + (1.0 - mixing) * new_global[None]
    forward_weight = mixed[:, :D].astype(jnp.bfloat16)
    return (mixed, first_moment, second_moment, new_global, new_mom, forward_weight)
```

```python
import jax
import jax.numpy as jnp
from jax import lax
from jax.sharding import Mesh
from jax.sharding import PartitionSpec as P

INNER_STEP = 100


beta_one = 0.9
beta_two = 0.95
epsilon = 1e-08
inner_rate = 0.001
decay_rate = 0.1
outer_rate = 0.7
momentum = 0.9
mixing = 0.5

X, Y_LO, Z, Y_HI, CORE = 4, 2, 12, 4, 2
PLANE = ("x", "y_lo")
FSDP = ("x", "y_lo", "z")
ISLAND = ("y_hi", "core")


def to_every(block, axes, count):
    copies = jnp.broadcast_to(block[None], (count, *block.shape))
    return lax.all_to_all(copies, axes, 0, 0)


def on_device(acts, grad_out, params, adam_m, adam_v, global_params, outer_mom):
    shard_rows = params.shape[1]
    features = acts.shape[2]
    width = params.shape[2]
    plane, islands = X * Y_LO, Y_HI * CORE
    padded_rows = shard_rows * plane * Z
    whole = jnp.einsum("td,th->dh", acts[0], grad_out[0], preferred_element_type=jnp.float32)
    whole = jnp.pad(whole, ((0, padded_rows - features), (0, 0)))
    sent = whole.reshape(plane, Z * shard_rows, width).astype(jnp.float16)
    got = lax.all_to_all(sent, PLANE, 0, 0)
    part = jnp.sum(got.astype(jnp.float32), axis=0)
    sent = part.reshape(Z, shard_rows, width).astype(jnp.float16)
    got = lax.all_to_all(sent, "z", 0, 0)
    gradient = jnp.sum(got.astype(jnp.float32), axis=0)
    first_moment = beta_one * adam_m[0] + (1.0 - beta_one) * gradient
    second_moment = beta_two * adam_v[0] + (1.0 - beta_two) * gradient * gradient
    first_hat = first_moment / (1.0 - beta_one**INNER_STEP)
    second_hat = second_moment / (1.0 - beta_two**INNER_STEP)
    inner = params[0] - inner_rate * (
        first_hat / (jnp.sqrt(second_hat) + epsilon) + decay_rate * params[0]
    )
    summed = jnp.sum(to_every(global_params - inner, ISLAND, islands), axis=0)
    delta = summed / islands
    new_mom = momentum * outer_mom + delta
    new_global = global_params - outer_rate * (delta + momentum * new_mom)
    mixed = mixing * inner + (1.0 - mixing) * new_global
    column = to_every(mixed.astype(jnp.bfloat16), "z", Z).reshape(Z * shard_rows, width)
    gathered = to_every(column, PLANE, plane).reshape(padded_rows, width)
    forward_weight = gathered[:features]
    return (
        mixed[None],
        first_moment[None],
        second_moment[None],
        new_global,
        new_mom,
        forward_weight[None],
    )


def solution(mesh):
    grid = Mesh(mesh.devices.reshape(X, Y_LO, Z, Y_HI, CORE), (*FSDP, *ISLAND))
    in_specs = (
        P(ISLAND, FSDP, None),
        P(ISLAND, FSDP, None),
        P(ISLAND, FSDP, None),
        P(ISLAND, FSDP, None),
        P(ISLAND, FSDP, None),
        P(FSDP, None),
        P(FSDP, None),
    )
    out_specs = (
        P(ISLAND, FSDP, None),
        P(ISLAND, FSDP, None),
        P(ISLAND, FSDP, None),
        P(FSDP, None),
        P(FSDP, None),
        P(ISLAND, None, None),
    )
    return jax.shard_map(
        on_device, mesh=grid, in_specs=in_specs, out_specs=out_specs, check_vma=False
    )
```

```python
import functools
import jax
import jax.numpy as jnp
from jax import lax
from jax.experimental import pallas as pl
from jax.experimental.pallas import tpu as pltpu
from jax.sharding import Mesh
from jax.sharding import PartitionSpec as P

INNER_STEP = 100


beta_one = 0.9
beta_two = 0.95
epsilon = 1e-08
inner_rate = 0.001
decay_rate = 0.1
outer_rate = 0.7
momentum = 0.9
mixing = 0.5

X, Y_LO, Z, Y_HI, CORE = 4, 2, 12, 4, 2
PLANE = ("x", "y_lo")
FSDP = ("x", "y_lo", "z")
ISLAND = ("y_hi", "core")


def to_every(block, axes, count):
    copies = jnp.broadcast_to(block[None], (count, *block.shape))
    return lax.all_to_all(copies, axes, 0, 0)


def product_kernel(rows, acts_hbm, cot_hbm, out_ref, acts, cot, whole, arrived, cot_arrived):
    tokens, features = acts_hbm.shape
    blocks = out_ref.shape[0]
    step = features // blocks
    copies = [
        pltpu.make_async_copy(
            acts_hbm.at[:, pl.ds(j * step, step)], acts.at[:, pl.ds(j * step, step)], arrived.at[j]
        )
        for j in range(blocks)
    ]
    cot_copy = pltpu.make_async_copy(cot_hbm, cot, cot_arrived)
    cot_copy.start()
    for copy in copies:
        copy.start()
    whole[pl.ds(features, whole.shape[0] - features), :] = jnp.zeros(
        (whole.shape[0] - features, whole.shape[1]), jnp.float32
    )
    cot_copy.wait()
    for j, copy in enumerate(copies):
        copy.wait()
        whole[pl.ds(j * step, step), :] = lax.dot_general(
            acts[:, pl.ds(j * step, step)],
            cot[...],
            (((0,), (0,)), ((), ())),
            preferred_element_type=jnp.float32,
        )
        if j > 0:
            out_ref[j - 1] = whole[pl.ds((j - 1) * rows, rows), :].astype(out_ref.dtype)
    out_ref[blocks - 1] = whole[pl.ds((blocks - 1) * rows, rows), :].astype(out_ref.dtype)


def product(acts, cot, blocks, rows):
    tokens, features = acts.shape
    width = cot.shape[1]
    return pl.pallas_call(
        functools.partial(product_kernel, rows),
        out_shape=jax.ShapeDtypeStruct((blocks, rows, width), jnp.float32),
        in_specs=[pl.BlockSpec(memory_space=pltpu.HBM)] * 2,
        out_specs=pl.BlockSpec(memory_space=pltpu.VMEM),
        scratch_shapes=[
            pltpu.VMEM((tokens, features), acts.dtype),
            pltpu.VMEM((tokens, width), cot.dtype),
            pltpu.VMEM((-(-blocks * rows // 8) * 8, width), jnp.float32),
            pltpu.SemaphoreType.DMA((blocks,)),
            pltpu.SemaphoreType.DMA(()),
        ],
        compiler_params=pltpu.CompilerParams(vmem_limit_bytes=12 << 20),
        name="product",
    )(*(pltpu.with_memory_space_constraint(a, pltpu.HBM) for a in (acts, cot)))


def finish_kernel(rows, tall, *refs):
    small = (len(refs) - 5) // 2
    blocks_ref, arrays, out_hbm = refs[0], refs[1 : small + 1], refs[small + 1]
    outs = refs[small + 2 : 2 * small + 2]
    joined, upright, left = refs[2 * small + 2 :]
    blocks = blocks_ref.shape[0]
    step = out_hbm.shape[0] // blocks
    copies = []

    def send(source, target):
        copies.append(pltpu.make_async_copy(source, target, left.at[len(copies)]))
        copies[-1].start()

    for j in range(blocks):
        first = j * step
        while first < (j + 1) * step:
            b = first // rows
            last = min((j + 1) * step, (b + 1) * rows)
            joined[pl.ds(first, last - first), :] = blocks_ref[b, pl.ds(first - b * rows, last - first), :]
            first = last
        send(joined.at[pl.ds(j * step, step)], out_hbm.at[pl.ds(j * step, step)])
    for i in range(small):
        if i < tall:
            upright[i, :, 0, :] = arrays[i][...]
            send(upright.at[i], outs[i])
        else:
            send(arrays[i], outs[i])
    for copy in copies:
        copy.wait()


def finish(blocks, features, tall, flat):
    count, rows, width = blocks.shape
    shard_rows = tall[0].shape[0]
    arrays = (*tall, *flat)
    f32 = jnp.float32
    out = pl.pallas_call(
        functools.partial(finish_kernel, rows, len(tall)),
        out_shape=[
            jax.ShapeDtypeStruct((features, width), blocks.dtype),
            *[jax.ShapeDtypeStruct((shard_rows, 1, width), f32) for _ in tall],
            *[jax.ShapeDtypeStruct((shard_rows, width), f32) for _ in flat],
        ],
        in_specs=[pl.BlockSpec(memory_space=pltpu.VMEM)] * (1 + len(arrays)),
        out_specs=[pl.BlockSpec(memory_space=pltpu.HBM)] * (1 + len(arrays)),
        scratch_shapes=[
            pltpu.VMEM((features, width), blocks.dtype),
            pltpu.VMEM((len(tall), shard_rows, 1, width), f32),
            pltpu.SemaphoreType.DMA((count + len(arrays),)),
        ],
        compiler_params=pltpu.CompilerParams(vmem_limit_bytes=4 << 20),
        name="finish",
    )(blocks, *arrays)
    return out[0], [jnp.swapaxes(a, 0, 1) for a in out[1 : 1 + len(tall)]], out[1 + len(tall) :]


def on_device(acts, grad_out, params, adam_m, adam_v, global_params, outer_mom):
    shard_rows = params.shape[1]
    features = acts.shape[2]
    width = params.shape[2]
    plane, islands = X * Y_LO, Y_HI * CORE
    sent = product(acts[0], grad_out[0], plane, Z * shard_rows).astype(jnp.float16)
    got = lax.all_to_all(sent, PLANE, 0, 0)
    part = jnp.sum(got.astype(jnp.float32), axis=0)
    sent = part.reshape(Z, shard_rows, width).astype(jnp.float16)
    got = lax.all_to_all(sent, "z", 0, 0)
    gradient = jnp.sum(got.astype(jnp.float32), axis=0)
    first_moment = beta_one * adam_m[0] + (1.0 - beta_one) * gradient
    second_moment = beta_two * adam_v[0] + (1.0 - beta_two) * gradient * gradient
    first_hat = first_moment / (1.0 - beta_one**INNER_STEP)
    second_hat = second_moment / (1.0 - beta_two**INNER_STEP)
    inner = params[0] - inner_rate * (
        first_hat / (jnp.sqrt(second_hat) + epsilon) + decay_rate * params[0]
    )
    summed = jnp.sum(to_every(global_params - inner, ISLAND, islands), axis=0)
    delta = summed / islands
    new_mom = momentum * outer_mom + delta
    new_global = global_params - outer_rate * (delta + momentum * new_mom)
    mixed = mixing * inner + (1.0 - mixing) * new_global
    column = to_every(mixed.astype(jnp.bfloat16), "z", Z).reshape(Z * shard_rows, width)
    forward_weight, tall, flat = finish(
        to_every(column, PLANE, plane),
        features,
        (mixed, first_moment, second_moment),
        (new_global, new_mom),
    )
    return (*tall, *flat, forward_weight[None])


def solution(mesh):
    grid = Mesh(mesh.devices.reshape(X, Y_LO, Z, Y_HI, CORE), (*FSDP, *ISLAND))
    in_specs = (
        P(ISLAND, FSDP, None),
        P(ISLAND, FSDP, None),
        P(ISLAND, FSDP, None),
        P(ISLAND, FSDP, None),
        P(ISLAND, FSDP, None),
        P(FSDP, None),
        P(FSDP, None),
    )
    out_specs = (
        P(ISLAND, FSDP, None),
        P(ISLAND, FSDP, None),
        P(ISLAND, FSDP, None),
        P(FSDP, None),
        P(FSDP, None),
        P(ISLAND, None, None),
    )
    return jax.shard_map(
        on_device, mesh=grid, in_specs=in_specs, out_specs=out_specs, check_vma=False
    )
```

```python
import functools
import jax
import jax.numpy as jnp
from jax import lax
from jax.experimental import pallas as pl
from jax.experimental.pallas import tpu as pltpu
from jax.sharding import Mesh
from jax.sharding import PartitionSpec as P

INNER_STEP = 100


beta_one = 0.9
beta_two = 0.95
epsilon = 1e-08
inner_rate = 0.001
decay_rate = 0.1
outer_rate = 0.7
momentum = 0.9
mixing = 0.5

X, Y_LO, Z, Y_HI, CORE = 4, 2, 12, 4, 2
STEPS = 2
PLANE = ("x", "y_lo")
FSDP = ("x", "y_lo", "z")
ISLAND = ("y_hi", "core")


def to_every(block, axes, count):
    copies = jnp.broadcast_to(block[None], (count, *block.shape))
    return lax.all_to_all(copies, axes, 0, 0)


def product_kernel(acts_hbm, cot_hbm, out_ref, acts, cot, arrived, cot_arrived):
    features = acts_hbm.shape[1]
    blocks, rows, width = out_ref.shape
    step = features // STEPS
    cot_copy = pltpu.make_async_copy(cot_hbm, cot, cot_arrived)
    cot_copy.start()
    copies = [
        pltpu.make_async_copy(
            acts_hbm.at[:, pl.ds(j * step, step)], acts.at[:, pl.ds(j * step, step)], arrived.at[j]
        )
        for j in range(STEPS)
    ]
    for copy in copies:
        copy.start()
    past = features - (blocks - 1) * rows
    out_ref[blocks - 1, pl.ds(past, rows - past), :] = jnp.zeros((rows - past, width), jnp.float32)
    cot_copy.wait()
    for j, copy in enumerate(copies):
        copy.wait()
        part = lax.dot_general(
            cot[...],
            acts[:, pl.ds(j * step, step)],
            (((0,), (0,)), ((), ())),
            preferred_element_type=jnp.float32,
        ).T
        first = j * step
        while first < (j + 1) * step:
            b = first // rows
            last = min((b + 1) * rows, (j + 1) * step)
            if first % 8:
                last = min(last, -(-first // 8) * 8)
            out_ref[b, pl.ds(first - b * rows, last - first), :] = part[first - j * step : last - j * step]
            first = last


def product(acts, cot, blocks, rows):
    tokens, features = acts.shape
    width = cot.shape[1]
    return pl.pallas_call(
        product_kernel,
        out_shape=jax.ShapeDtypeStruct((blocks, rows, width), jnp.float32),
        in_specs=[pl.BlockSpec(memory_space=pltpu.HBM)] * 2,
        out_specs=pl.BlockSpec(memory_space=pltpu.VMEM),
        scratch_shapes=[
            pltpu.VMEM((tokens, features), acts.dtype),
            pltpu.VMEM((tokens, width), cot.dtype),
            pltpu.SemaphoreType.DMA((STEPS,)),
            pltpu.SemaphoreType.DMA(()),
        ],
        compiler_params=pltpu.CompilerParams(vmem_limit_bytes=8 << 20),
        name="product",
    )(*(pltpu.with_memory_space_constraint(a, pltpu.HBM) for a in (acts, cot)))


def finish_kernel(rows, tall, *refs):
    small = (len(refs) - 5) // 2
    blocks_ref, arrays, out_hbm = refs[0], refs[1 : small + 1], refs[small + 1]
    outs = refs[small + 2 : 2 * small + 2]
    joined, upright, left = refs[2 * small + 2 :]
    blocks = blocks_ref.shape[0]
    step = out_hbm.shape[0] // blocks
    copies = []

    def send(source, target):
        copies.append(pltpu.make_async_copy(source, target, left.at[len(copies)]))
        copies[-1].start()

    for j in range(blocks):
        first = j * step
        while first < (j + 1) * step:
            b = first // rows
            last = min((j + 1) * step, (b + 1) * rows)
            joined[pl.ds(first, last - first), :] = blocks_ref[b, pl.ds(first - b * rows, last - first), :]
            first = last
        send(joined.at[pl.ds(j * step, step)], out_hbm.at[pl.ds(j * step, step)])
    for i in range(small):
        if i < tall:
            upright[i, :, 0, :] = arrays[i][...]
            send(upright.at[i], outs[i])
        else:
            send(arrays[i], outs[i])
    for copy in copies:
        copy.wait()


def finish(blocks, features, tall, flat):
    count, rows, width = blocks.shape
    shard_rows = tall[0].shape[0]
    arrays = (*tall, *flat)
    f32 = jnp.float32
    out = pl.pallas_call(
        functools.partial(finish_kernel, rows, len(tall)),
        out_shape=[
            jax.ShapeDtypeStruct((features, width), blocks.dtype),
            *[jax.ShapeDtypeStruct((shard_rows, 1, width), f32) for _ in tall],
            *[jax.ShapeDtypeStruct((shard_rows, width), f32) for _ in flat],
        ],
        in_specs=[pl.BlockSpec(memory_space=pltpu.VMEM)] * (1 + len(arrays)),
        out_specs=[pl.BlockSpec(memory_space=pltpu.HBM)] * (1 + len(arrays)),
        scratch_shapes=[
            pltpu.VMEM((features, width), blocks.dtype),
            pltpu.VMEM((len(tall), shard_rows, 1, width), f32),
            pltpu.SemaphoreType.DMA((count + len(arrays),)),
        ],
        compiler_params=pltpu.CompilerParams(vmem_limit_bytes=4 << 20),
        name="finish",
    )(blocks, *arrays)
    return out[0], [jnp.swapaxes(a, 0, 1) for a in out[1 : 1 + len(tall)]], out[1 + len(tall) :]


def on_device(acts, grad_out, params, adam_m, adam_v, global_params, outer_mom):
    shard_rows = params.shape[1]
    features = acts.shape[2]
    width = params.shape[2]
    plane, islands = X * Y_LO, Y_HI * CORE
    sent = product(acts[0], grad_out[0], plane, Z * shard_rows).astype(jnp.float16)
    got = lax.all_to_all(sent, PLANE, 0, 0)
    part = jnp.sum(got.astype(jnp.float32), axis=0)
    sent = part.reshape(Z, shard_rows, width).astype(jnp.float16)
    got = lax.all_to_all(sent, "z", 0, 0)
    gradient = jnp.sum(got.astype(jnp.float32), axis=0)
    first_moment = beta_one * adam_m[0] + (1.0 - beta_one) * gradient
    second_moment = beta_two * adam_v[0] + (1.0 - beta_two) * gradient * gradient
    first_hat = first_moment / (1.0 - beta_one**INNER_STEP)
    second_hat = second_moment / (1.0 - beta_two**INNER_STEP)
    inner = params[0] - inner_rate * (
        first_hat / (jnp.sqrt(second_hat) + epsilon) + decay_rate * params[0]
    )
    summed = jnp.sum(to_every(global_params - inner, ISLAND, islands), axis=0)
    delta = summed / islands
    new_mom = momentum * outer_mom + delta
    new_global = global_params - outer_rate * (delta + momentum * new_mom)
    mixed = mixing * inner + (1.0 - mixing) * new_global
    column = to_every(mixed.astype(jnp.bfloat16), "z", Z).reshape(Z * shard_rows, width)
    forward_weight, tall, flat = finish(
        to_every(column, PLANE, plane),
        features,
        (mixed, first_moment, second_moment),
        (new_global, new_mom),
    )
    return (*tall, *flat, forward_weight[None])


def solution(mesh):
    grid = Mesh(mesh.devices.reshape(X, Y_LO, Z, Y_HI, CORE), (*FSDP, *ISLAND))
    in_specs = (
        P(ISLAND, FSDP, None),
        P(ISLAND, FSDP, None),
        P(ISLAND, FSDP, None),
        P(ISLAND, FSDP, None),
        P(ISLAND, FSDP, None),
        P(FSDP, None),
        P(FSDP, None),
    )
    out_specs = (
        P(ISLAND, FSDP, None),
        P(ISLAND, FSDP, None),
        P(ISLAND, FSDP, None),
        P(FSDP, None),
        P(FSDP, None),
        P(ISLAND, None, None),
    )
    return jax.shard_map(
        on_device, mesh=grid, in_specs=in_specs, out_specs=out_specs, check_vma=False
    )
```

```python
import functools
import jax
import jax.numpy as jnp
from jax import lax
from jax.experimental import pallas as pl
from jax.experimental.pallas import tpu as pltpu
from jax.sharding import Mesh
from jax.sharding import PartitionSpec as P

INNER_STEP = 100


beta_one = 0.9
beta_two = 0.95
epsilon = 1e-08
inner_rate = 0.001
decay_rate = 0.1
outer_rate = 0.7
momentum = 0.9
mixing = 0.5

X, Y_LO, Z = 4, 2, 12
STEPS = 2
PLANE = X * Y_LO
FSDP = ("plane", "z")


def exchange(blocks, axis, turned=False):
    members = list(range(blocks.shape[0]))
    groups = [members[::-1]] if turned else None
    return lax.all_to_all(blocks, axis, 0, 0, axis_index_groups=groups)


def copies_of(block, count):
    return jnp.broadcast_to(block[None], (count, *block.shape))


def product_kernel(acts_hbm, cot_hbm, out_ref, acts, cot, arrived, cot_arrived):
    features = acts_hbm.shape[1]
    blocks, rows, width = out_ref.shape
    step = features // STEPS
    cot_copy = pltpu.make_async_copy(cot_hbm, cot, cot_arrived)
    cot_copy.start()
    copies = [
        pltpu.make_async_copy(
            acts_hbm.at[:, pl.ds(j * step, step)], acts.at[:, pl.ds(j * step, step)], arrived.at[j]
        )
        for j in range(STEPS)
    ]
    for copy in copies:
        copy.start()
    past = features - (blocks - 1) * rows
    out_ref[blocks - 1, pl.ds(past, rows - past), :] = jnp.zeros((rows - past, width), jnp.float32)
    cot_copy.wait()
    for j, copy in enumerate(copies):
        copy.wait()
        part = lax.dot_general(
            cot[...],
            acts[:, pl.ds(j * step, step)],
            (((0,), (0,)), ((), ())),
            preferred_element_type=jnp.float32,
        ).T
        first = j * step
        while first < (j + 1) * step:
            b = first // rows
            last = min((b + 1) * rows, (j + 1) * step)
            if first % 8:
                last = min(last, -(-first // 8) * 8)
            out_ref[b, pl.ds(first - b * rows, last - first), :] = part[first - j * step : last - j * step]
            first = last


def product(acts, cot, blocks, rows):
    tokens, features = acts.shape
    width = cot.shape[1]
    return pl.pallas_call(
        product_kernel,
        out_shape=jax.ShapeDtypeStruct((blocks, rows, width), jnp.float32),
        in_specs=[pl.BlockSpec(memory_space=pltpu.HBM)] * 2,
        out_specs=pl.BlockSpec(memory_space=pltpu.VMEM),
        scratch_shapes=[
            pltpu.VMEM((tokens, features), acts.dtype),
            pltpu.VMEM((tokens, width), cot.dtype),
            pltpu.SemaphoreType.DMA((STEPS,)),
            pltpu.SemaphoreType.DMA(()),
        ],
        compiler_params=pltpu.CompilerParams(vmem_limit_bytes=8 << 20),
        name="product",
    )(*(pltpu.with_memory_space_constraint(a, pltpu.HBM) for a in (acts, cot)))


def finish_kernel(rows, tall, *refs):
    small = (len(refs) - 5) // 2
    blocks_ref, arrays, out_hbm = refs[0], refs[1 : small + 1], refs[small + 1]
    outs = refs[small + 2 : 2 * small + 2]
    joined, upright, left = refs[2 * small + 2 :]
    blocks = blocks_ref.shape[0]
    step = out_hbm.shape[0] // blocks
    copies = []

    def send(source, target):
        copies.append(pltpu.make_async_copy(source, target, left.at[len(copies)]))
        copies[-1].start()

    for j in range(blocks):
        first = j * step
        while first < (j + 1) * step:
            b = first // rows
            last = min((j + 1) * step, (b + 1) * rows)
            joined[pl.ds(first, last - first), :] = blocks_ref[b, pl.ds(first - b * rows, last - first), :]
            first = last
        send(joined.at[pl.ds(j * step, step)], out_hbm.at[pl.ds(j * step, step)])
    for i in range(small):
        if i < tall:
            upright[i, :, 0, :] = arrays[i][...]
            send(upright.at[i], outs[i])
        else:
            send(arrays[i], outs[i])
    for copy in copies:
        copy.wait()


def finish(blocks, features, tall, flat):
    count, rows, width = blocks.shape
    shard_rows = tall[0].shape[0]
    arrays = (*tall, *flat)
    f32 = jnp.float32
    out = pl.pallas_call(
        functools.partial(finish_kernel, rows, len(tall)),
        out_shape=[
            jax.ShapeDtypeStruct((features, width), blocks.dtype),
            *[jax.ShapeDtypeStruct((shard_rows, 1, width), f32) for _ in tall],
            *[jax.ShapeDtypeStruct((shard_rows, width), f32) for _ in flat],
        ],
        in_specs=[pl.BlockSpec(memory_space=pltpu.VMEM)] * (1 + len(arrays)),
        out_specs=[pl.BlockSpec(memory_space=pltpu.HBM)] * (1 + len(arrays)),
        scratch_shapes=[
            pltpu.VMEM((features, width), blocks.dtype),
            pltpu.VMEM((len(tall), shard_rows, 1, width), f32),
            pltpu.SemaphoreType.DMA((count + len(arrays),)),
        ],
        compiler_params=pltpu.CompilerParams(vmem_limit_bytes=4 << 20),
        name="finish",
    )(blocks, *arrays)
    return out[0], [jnp.swapaxes(a, 0, 1) for a in out[1 : 1 + len(tall)]], out[1 + len(tall) :]


def on_device(acts, grad_out, params, adam_m, adam_v, global_params, outer_mom):
    shard_rows = params.shape[1]
    features = acts.shape[2]
    width = params.shape[2]
    islands = lax.axis_size("island")
    sent = product(acts[0], grad_out[0], PLANE, Z * shard_rows).astype(jnp.float16)
    got = exchange(sent, "plane")
    part = jnp.sum(got.astype(jnp.float32), axis=0)
    sent = part.reshape(Z, shard_rows, width).astype(jnp.float16)
    got = exchange(sent[::-1], "z", turned=True)
    gradient = jnp.sum(got.astype(jnp.float32), axis=0)
    first_moment = beta_one * adam_m[0] + (1.0 - beta_one) * gradient
    second_moment = beta_two * adam_v[0] + (1.0 - beta_two) * gradient * gradient
    first_hat = first_moment / (1.0 - beta_one**INNER_STEP)
    second_hat = second_moment / (1.0 - beta_two**INNER_STEP)
    inner = params[0] - inner_rate * (
        first_hat / (jnp.sqrt(second_hat) + epsilon) + decay_rate * params[0]
    )
    summed = jnp.sum(exchange(copies_of(global_params - inner, islands), "island", turned=True)[::-1], axis=0)
    delta = summed / islands
    new_mom = momentum * outer_mom + delta
    new_global = global_params - outer_rate * (delta + momentum * new_mom)
    mixed = mixing * inner + (1.0 - mixing) * new_global
    column = exchange(copies_of(mixed.astype(jnp.bfloat16), Z), "z", turned=True)[::-1]
    column = column.reshape(Z * shard_rows, width)
    forward_weight, tall, flat = finish(
        exchange(copies_of(column, PLANE), "plane"),
        features,
        (mixed, first_moment, second_moment),
        (new_global, new_mom),
    )
    return (*tall, *flat, forward_weight[None])


def solution(mesh):
    grid = Mesh(mesh.devices.reshape(PLANE, Z, -1), (*FSDP, "island"))
    in_specs = (
        P("island", FSDP, None),
        P("island", FSDP, None),
        P("island", FSDP, None),
        P("island", FSDP, None),
        P("island", FSDP, None),
        P(FSDP, None),
        P(FSDP, None),
    )
    out_specs = (
        P("island", FSDP, None),
        P("island", FSDP, None),
        P("island", FSDP, None),
        P(FSDP, None),
        P(FSDP, None),
        P("island", None, None),
    )
    return jax.shard_map(
        on_device, mesh=grid, in_specs=in_specs, out_specs=out_specs, check_vma=False
    )
```

```python
import functools
import jax
import jax.numpy as jnp
from jax import lax
from jax.experimental import pallas as pl
from jax.experimental.pallas import tpu as pltpu
from jax.sharding import Mesh
from jax.sharding import PartitionSpec as P

INNER_STEP = 100


beta_one = 0.9
beta_two = 0.95
epsilon = 1e-08
inner_rate = 0.001
decay_rate = 0.1
outer_rate = 0.7
momentum = 0.9
mixing = 0.5

X, Y_LO, Z = 4, 2, 12
STEPS = 2
PLANE = X * Y_LO
FSDP = ("plane", "z")


def exchange(blocks, axis, turned=False):
    members = list(range(blocks.shape[0]))
    groups = [members[::-1]] if turned else None
    return lax.all_to_all(blocks, axis, 0, 0, axis_index_groups=groups)


def exchange_z(listed):
    half = Z // 2
    groups = [[z for near in range(half) for z in (Z - 1 - near, half - 1 - near)]]
    return lax.all_to_all(listed, "z", 0, 0, axis_index_groups=groups)


def listed_z(blocks):
    shape = blocks.shape[1:]
    return jnp.swapaxes(blocks[::-1].reshape(2, Z // 2, *shape), 0, 1).reshape(Z, *shape)


def unlisted_z(listed):
    shape = listed.shape[1:]
    return jnp.swapaxes(listed.reshape(Z // 2, 2, *shape), 0, 1).reshape(Z, *shape)[::-1]


def copies_of(block, count):
    return jnp.broadcast_to(block[None], (count, *block.shape))


def product_kernel(acts_hbm, cot_hbm, out_ref, acts, cot, arrived, cot_arrived):
    features = acts_hbm.shape[1]
    blocks, rows, width = out_ref.shape
    step = features // STEPS
    cot_copy = pltpu.make_async_copy(cot_hbm, cot, cot_arrived)
    cot_copy.start()
    copies = [
        pltpu.make_async_copy(
            acts_hbm.at[:, pl.ds(j * step, step)], acts.at[:, pl.ds(j * step, step)], arrived.at[j]
        )
        for j in range(STEPS)
    ]
    for copy in copies:
        copy.start()
    past = features - (blocks - 1) * rows
    out_ref[blocks - 1, pl.ds(past, rows - past), :] = jnp.zeros((rows - past, width), jnp.float32)
    cot_copy.wait()
    for j, copy in enumerate(copies):
        copy.wait()
        part = lax.dot_general(
            cot[...],
            acts[:, pl.ds(j * step, step)],
            (((0,), (0,)), ((), ())),
            preferred_element_type=jnp.float32,
        ).T
        first = j * step
        while first < (j + 1) * step:
            b = first // rows
            last = min((b + 1) * rows, (j + 1) * step)
            if first % 8:
                last = min(last, -(-first // 8) * 8)
            out_ref[b, pl.ds(first - b * rows, last - first), :] = part[first - j * step : last - j * step]
            first = last


def product(acts, cot, blocks, rows):
    tokens, features = acts.shape
    width = cot.shape[1]
    return pl.pallas_call(
        product_kernel,
        out_shape=jax.ShapeDtypeStruct((blocks, rows, width), jnp.float32),
        in_specs=[pl.BlockSpec(memory_space=pltpu.HBM)] * 2,
        out_specs=pl.BlockSpec(memory_space=pltpu.VMEM),
        scratch_shapes=[
            pltpu.VMEM((tokens, features), acts.dtype),
            pltpu.VMEM((tokens, width), cot.dtype),
            pltpu.SemaphoreType.DMA((STEPS,)),
            pltpu.SemaphoreType.DMA(()),
        ],
        compiler_params=pltpu.CompilerParams(vmem_limit_bytes=8 << 20),
        name="product",
    )(*(pltpu.with_memory_space_constraint(a, pltpu.HBM) for a in (acts, cot)))


def finish_kernel(rows, tall, *refs):
    small = (len(refs) - 5) // 2
    blocks_ref, arrays, out_hbm = refs[0], refs[1 : small + 1], refs[small + 1]
    outs = refs[small + 2 : 2 * small + 2]
    joined, upright, left = refs[2 * small + 2 :]
    blocks = blocks_ref.shape[0]
    step = out_hbm.shape[0] // blocks
    copies = []

    def send(source, target):
        copies.append(pltpu.make_async_copy(source, target, left.at[len(copies)]))
        copies[-1].start()

    for j in range(blocks):
        first = j * step
        while first < (j + 1) * step:
            b = first // rows
            last = min((j + 1) * step, (b + 1) * rows)
            joined[pl.ds(first, last - first), :] = blocks_ref[blocks - 1 - b, pl.ds(first - b * rows, last - first), :]
            first = last
        send(joined.at[pl.ds(j * step, step)], out_hbm.at[pl.ds(j * step, step)])
    for i in range(small):
        if i < tall:
            upright[i, :, 0, :] = arrays[i][...]
            send(upright.at[i], outs[i])
        else:
            send(arrays[i], outs[i])
    for copy in copies:
        copy.wait()


def finish(blocks, features, tall, flat):
    count, rows, width = blocks.shape
    shard_rows = tall[0].shape[0]
    arrays = (*tall, *flat)
    f32 = jnp.float32
    out = pl.pallas_call(
        functools.partial(finish_kernel, rows, len(tall)),
        out_shape=[
            jax.ShapeDtypeStruct((features, width), blocks.dtype),
            *[jax.ShapeDtypeStruct((shard_rows, 1, width), f32) for _ in tall],
            *[jax.ShapeDtypeStruct((shard_rows, width), f32) for _ in flat],
        ],
        in_specs=[pl.BlockSpec(memory_space=pltpu.VMEM)] * (1 + len(arrays)),
        out_specs=[pl.BlockSpec(memory_space=pltpu.HBM)] * (1 + len(arrays)),
        scratch_shapes=[
            pltpu.VMEM((features, width), blocks.dtype),
            pltpu.VMEM((len(tall), shard_rows, 1, width), f32),
            pltpu.SemaphoreType.DMA((count + len(arrays),)),
        ],
        compiler_params=pltpu.CompilerParams(vmem_limit_bytes=4 << 20),
        name="finish",
    )(blocks, *arrays)
    return out[0], [jnp.swapaxes(a, 0, 1) for a in out[1 : 1 + len(tall)]], out[1 + len(tall) :]


def on_device(acts, grad_out, params, adam_m, adam_v, global_params, outer_mom):
    shard_rows = params.shape[1]
    features = acts.shape[2]
    width = params.shape[2]
    islands = lax.axis_size("island")
    sent = product(acts[0], grad_out[0], PLANE, Z * shard_rows).astype(jnp.float16)
    got = exchange(sent, "plane")
    part = jnp.sum(got.astype(jnp.float32), axis=0)
    sent = part.reshape(Z, shard_rows, width).astype(jnp.float16)
    got = exchange_z(listed_z(sent))
    gradient = jnp.sum(got.astype(jnp.float32), axis=0)
    first_moment = beta_one * adam_m[0] + (1.0 - beta_one) * gradient
    second_moment = beta_two * adam_v[0] + (1.0 - beta_two) * gradient * gradient
    first_hat = first_moment / (1.0 - beta_one**INNER_STEP)
    second_hat = second_moment / (1.0 - beta_two**INNER_STEP)
    inner = params[0] - inner_rate * (
        first_hat / (jnp.sqrt(second_hat) + epsilon) + decay_rate * params[0]
    )
    summed = jnp.sum(exchange(copies_of(global_params - inner, islands), "island", turned=True)[::-1], axis=0)
    delta = summed / islands
    new_mom = momentum * outer_mom + delta
    new_global = global_params - outer_rate * (delta + momentum * new_mom)
    mixed = mixing * inner + (1.0 - mixing) * new_global
    column = unlisted_z(exchange_z(copies_of(mixed.astype(jnp.bfloat16), Z)))
    column = column.reshape(Z * shard_rows, width)
    forward_weight, tall, flat = finish(
        exchange(copies_of(column, PLANE), "plane", turned=True),
        features,
        (mixed, first_moment, second_moment),
        (new_global, new_mom),
    )
    return (*tall, *flat, forward_weight[None])


def solution(mesh):
    grid = Mesh(mesh.devices.reshape(PLANE, Z, -1), (*FSDP, "island"))
    in_specs = (
        P("island", FSDP, None),
        P("island", FSDP, None),
        P("island", FSDP, None),
        P("island", FSDP, None),
        P("island", FSDP, None),
        P(FSDP, None),
        P(FSDP, None),
    )
    out_specs = (
        P("island", FSDP, None),
        P("island", FSDP, None),
        P("island", FSDP, None),
        P(FSDP, None),
        P(FSDP, None),
        P("island", None, None),
    )
    return jax.shard_map(
        on_device, mesh=grid, in_specs=in_specs, out_specs=out_specs, check_vma=False
    )
```

```python
import functools
import jax
import jax.numpy as jnp
from jax import lax
from jax.experimental import pallas as pl
from jax.experimental.pallas import tpu as pltpu
from jax.sharding import Mesh
from jax.sharding import PartitionSpec as P

INNER_STEP = 100


beta_one = 0.9
beta_two = 0.95
epsilon = 1e-08
inner_rate = 0.001
decay_rate = 0.1
outer_rate = 0.7
momentum = 0.9
mixing = 0.5

X, Y_LO, Z = 4, 2, 12
STEPS = 2
PLANE = X * Y_LO
FSDP = ("plane", "z")


def exchange(blocks, axis, turned=False):
    members = list(range(blocks.shape[0]))
    groups = [members[::-1]] if turned else None
    return lax.all_to_all(blocks, axis, 0, 0, axis_index_groups=groups)


def exchange_z(listed):
    half = Z // 2
    groups = [[z for near in range(half) for z in (Z - 1 - near, half - 1 - near)]]
    return lax.all_to_all(listed, "z", 0, 0, axis_index_groups=groups)


def listed_z(blocks):
    shape = blocks.shape[1:]
    return jnp.swapaxes(blocks[::-1].reshape(2, Z // 2, *shape), 0, 1).reshape(Z, *shape)


def unlisted_z(listed):
    shape = listed.shape[1:]
    return jnp.swapaxes(listed.reshape(Z // 2, 2, *shape), 0, 1).reshape(Z, *shape)[::-1]


def copies_of(block, count):
    return jnp.broadcast_to(block[None], (count, *block.shape))


def product_kernel(acts_hbm, cot_hbm, out_ref, acts, cot, arrived, cot_arrived):
    features = acts_hbm.shape[1]
    blocks, rows, width = out_ref.shape
    step = features // STEPS
    cot_copy = pltpu.make_async_copy(cot_hbm, cot, cot_arrived)
    cot_copy.start()
    copies = [
        pltpu.make_async_copy(
            acts_hbm.at[:, pl.ds(j * step, step)], acts.at[:, pl.ds(j * step, step)], arrived.at[j]
        )
        for j in range(STEPS)
    ]
    for copy in copies:
        copy.start()
    past = features - (blocks - 1) * rows
    out_ref[blocks - 1, pl.ds(past, rows - past), :] = jnp.zeros((rows - past, width), jnp.float32)
    cot_copy.wait()
    for j, copy in enumerate(copies):
        copy.wait()
        part = lax.dot_general(
            cot[...],
            acts[:, pl.ds(j * step, step)],
            (((0,), (0,)), ((), ())),
            preferred_element_type=jnp.float32,
        ).T
        first = j * step
        while first < (j + 1) * step:
            b = first // rows
            last = min((b + 1) * rows, (j + 1) * step)
            if first % 8:
                last = min(last, -(-first // 8) * 8)
            out_ref[b, pl.ds(first - b * rows, last - first), :] = part[first - j * step : last - j * step]
            first = last


def product(acts, cot, blocks, rows):
    tokens, features = acts.shape
    width = cot.shape[1]
    return pl.pallas_call(
        product_kernel,
        out_shape=jax.ShapeDtypeStruct((blocks, rows, width), jnp.float32),
        in_specs=[pl.BlockSpec(memory_space=pltpu.HBM)] * 2,
        out_specs=pl.BlockSpec(memory_space=pltpu.VMEM),
        scratch_shapes=[
            pltpu.VMEM((tokens, features), acts.dtype),
            pltpu.VMEM((tokens, width), cot.dtype),
            pltpu.SemaphoreType.DMA((STEPS,)),
            pltpu.SemaphoreType.DMA(()),
        ],
        compiler_params=pltpu.CompilerParams(vmem_limit_bytes=8 << 20),
        name="product",
    )(*(pltpu.with_memory_space_constraint(a, pltpu.HBM) for a in (acts, cot)))


def finish_kernel(rows, tall, *refs):
    small = (len(refs) - 5) // 2
    blocks_ref, arrays, out_hbm = refs[0], refs[1 : small + 1], refs[small + 1]
    outs = refs[small + 2 : 2 * small + 2]
    joined, upright, left = refs[2 * small + 2 :]
    blocks = blocks_ref.shape[0]
    step = out_hbm.shape[0] // blocks
    copies = []

    def send(source, target):
        copies.append(pltpu.make_async_copy(source, target, left.at[len(copies)]))
        copies[-1].start()

    for i in range(small):
        if i < tall:
            upright[i, :, 0, :] = arrays[i][...]
            send(upright.at[i], outs[i])
        else:
            send(arrays[i], outs[i])
    for j in range(blocks):
        first = j * step
        while first < (j + 1) * step:
            b = first // rows
            last = min((j + 1) * step, (b + 1) * rows)
            joined[pl.ds(first, last - first), :] = blocks_ref[blocks - 1 - b, pl.ds(first - b * rows, last - first), :]
            first = last
        send(joined.at[pl.ds(j * step, step)], out_hbm.at[pl.ds(j * step, step)])
    for copy in copies:
        copy.wait()


def finish(blocks, features, tall, flat):
    count, rows, width = blocks.shape
    shard_rows = tall[0].shape[0]
    arrays = (*tall, *flat)
    f32 = jnp.float32
    out = pl.pallas_call(
        functools.partial(finish_kernel, rows, len(tall)),
        out_shape=[
            jax.ShapeDtypeStruct((features, width), blocks.dtype),
            *[jax.ShapeDtypeStruct((shard_rows, 1, width), f32) for _ in tall],
            *[jax.ShapeDtypeStruct((shard_rows, width), f32) for _ in flat],
        ],
        in_specs=[pl.BlockSpec(memory_space=pltpu.VMEM)] * (1 + len(arrays)),
        out_specs=[pl.BlockSpec(memory_space=pltpu.HBM)] * (1 + len(arrays)),
        scratch_shapes=[
            pltpu.VMEM((features, width), blocks.dtype),
            pltpu.VMEM((len(tall), shard_rows, 1, width), f32),
            pltpu.SemaphoreType.DMA((count + len(arrays),)),
        ],
        compiler_params=pltpu.CompilerParams(vmem_limit_bytes=4 << 20),
        name="finish",
    )(blocks, *arrays)
    return out[0], [jnp.swapaxes(a, 0, 1) for a in out[1 : 1 + len(tall)]], out[1 + len(tall) :]


def on_device(acts, grad_out, params, adam_m, adam_v, global_params, outer_mom):
    shard_rows = params.shape[1]
    features = acts.shape[2]
    width = params.shape[2]
    islands = lax.axis_size("island")
    sent = product(acts[0], grad_out[0], PLANE, Z * shard_rows).astype(jnp.float16)
    got = exchange(sent, "plane")
    part = jnp.sum(got.astype(jnp.float32), axis=0)
    sent = part.reshape(Z, shard_rows, width).astype(jnp.float16)
    got = exchange_z(listed_z(sent))
    gradient = jnp.sum(got.astype(jnp.float32), axis=0)
    first_moment = beta_one * adam_m[0] + (1.0 - beta_one) * gradient
    second_moment = beta_two * adam_v[0] + (1.0 - beta_two) * gradient * gradient
    first_hat = first_moment / (1.0 - beta_one**INNER_STEP)
    second_hat = second_moment / (1.0 - beta_two**INNER_STEP)
    inner = params[0] - inner_rate * (
        first_hat / (jnp.sqrt(second_hat) + epsilon) + decay_rate * params[0]
    )
    summed = jnp.sum(exchange(copies_of(global_params - inner, islands), "island", turned=True)[::-1], axis=0)
    delta = summed / islands
    new_mom = momentum * outer_mom + delta
    new_global = global_params - outer_rate * (delta + momentum * new_mom)
    mixed = mixing * inner + (1.0 - mixing) * new_global
    column = unlisted_z(exchange_z(copies_of(mixed.astype(jnp.bfloat16), Z)))
    column = column.reshape(Z * shard_rows, width)
    forward_weight, tall, flat = finish(
        exchange(copies_of(column, PLANE), "plane", turned=True),
        features,
        (mixed, first_moment, second_moment),
        (new_global, new_mom),
    )
    return (*tall, *flat, forward_weight[None])


def solution(mesh):
    grid = Mesh(mesh.devices.reshape(PLANE, Z, -1), (*FSDP, "island"))
    in_specs = (
        P("island", FSDP, None),
        P("island", FSDP, None),
        P("island", FSDP, None),
        P("island", FSDP, None),
        P("island", FSDP, None),
        P(FSDP, None),
        P(FSDP, None),
    )
    out_specs = (
        P("island", FSDP, None),
        P("island", FSDP, None),
        P("island", FSDP, None),
        P(FSDP, None),
        P(FSDP, None),
        P("island", None, None),
    )
    return jax.shard_map(
        on_device, mesh=grid, in_specs=in_specs, out_specs=out_specs, check_vma=False
    )
```
